32 devices in a mesh: grp: 4 (over y, x), freq: 8 (over z, core).
Axes of the slice: x: 2, y: 2, z: 4, core: 2. Of those that a mesh axis runs over, the one named last changes fastest.
Arguments:
- transfer: bfloat16 [512, 2, 128, 512], P('freq', None, 'grp'), may hold values from -0.1875 to 0.1875
- adjoint: bfloat16 [512, 2, 512, 128], P('freq'), may hold values from -6 to 6
- lower_rows: bfloat16 [131072, 384], P(('grp', 'freq')), may hold values from -6 to 6
- pivot_store: bfloat16 [512, 384], P('grp'), may hold values from -0.3125 to 0.3125
- owners: int32 [3], replicated, may hold values from 0 to 3
- inverse_factor: bfloat16 [128, 128], replicated, as said below
Outputs:
- panel: bfloat16 [131072, 128], P(('grp', 'freq'))
The draws below stay inside these ranges and needn't reach their ends.
Inputs may be any that keep to these rules, and one draw needn't show every extreme that they name: `inverse_factor`: upper triangular, with diagonal entries from 0.5 to 2.
All inputs are finite; a program needn't handle non-finite values.
Results may differ from the reference program's by a relative error of at most 0.0059.
Values may be sent and summed in bfloat16 or wider, within the bound.
A program may use at most 64 MiB of HBM per device.

```python
import math
import jax
import jax.numpy as jnp
from jax import lax

C = 128
M = 512
NF = 512
PANELS = 3
NT = 1024
NS = 128
N_GRP = 4


def draw_inverse_factor(key, part):
    key = jax.random.fold_in(key, 7)
    diag_key, upper_key = jax.random.split(key)
    diagonal = jnp.exp(jax.random.uniform(diag_key, (C,), jnp.float32, math.log(0.5), math.log(2.0)))
    upper_part = 0.5 * jax.random.normal(upper_key, (C, C), jnp.float32) / math.sqrt(C)
    return (jnp.triu(upper_part, 1) + jnp.diag(diagonal)).astype(jnp.bfloat16)


def block_levels(own_key, dims, pieces, least, high):
    loudness = 1.0
    for dim, shards_of in pieces:
        heights = jax.random.uniform(jax.random.fold_in(jax.random.fold_in(own_key, 6), dim), (shards_of,), jnp.float32, least / len(pieces), high / len(pieces))
        loudness = loudness * jnp.repeat(jnp.exp(heights), dims[dim] // shards_of).reshape((-1,) + (1,) * (len(dims) - 1 - dim))
    return loudness


def centred(own_key, shape, width, bound, cuts=(), kind=jnp.bfloat16):
    gain = block_levels(own_key, shape, cuts, -0.22, 0.18) if cuts else 1.0
    entries = jax.random.normal(own_key, shape, jnp.float32) * width * gain
    return jnp.minimum(jnp.maximum(entries, -bound), bound).astype(kind)


def setup_inputs(seed: int = 0) -> dict:
    key_list = jax.random.split(jax.random.key(seed), 7)
    transfer = centred(key_list[0], (NF, 2, NS, M), (2 * M) ** -0.5, 0.1875, ((0, 8), (2, 4)))
    adjoint = centred(key_list[1], (NF, 2, M, C), 1.0, 6.0, ((0, 8),))
    lower_rows = centred(key_list[2], (NS * NT, PANELS * C), 1.0, 6.0, ((0, 32),))
    pivot_store = centred(key_list[3], (C * N_GRP, PANELS * C), (PANELS * C) ** -0.5, 0.3125, ((0, 4),))
    owners = jax.random.randint(key_list[4], (PANELS,), 0, N_GRP).astype(jnp.int32)
    inverse_factor = draw_inverse_factor(jax.random.fold_in(key_list[6], 71), 0)
    return dict(transfer=transfer, adjoint=adjoint, lower_rows=lower_rows, pivot_store=pivot_store, owners=owners, inverse_factor=inverse_factor)


def make_table(samples, frequencies):
    time_steps = jnp.arange(samples, dtype=jnp.int32)[:, None]
    wave_numbers = jnp.arange(frequencies, dtype=jnp.int32)[None, :]
    phases = (time_steps * wave_numbers % samples).astype(jnp.float32) * (2.0 * math.pi / samples)
    factor = 1.0 / math.sqrt(frequencies)
    return jnp.stack([jnp.cos(phases) * factor, -jnp.sin(phases) * factor]).astype(jnp.bfloat16)

def spectrum(operands):
    trans_pair, adjoint_pair = operands
    trans_pair = trans_pair.astype(jnp.float32)
    adjoint_pair = adjoint_pair.astype(jnp.float32)
    highest = lax.Precision.HIGHEST
    real_part = jnp.dot(trans_pair[0], adjoint_pair[0], precision=highest) - jnp.dot(trans_pair[1], adjoint_pair[1], precision=highest)
    imag_part = jnp.dot(trans_pair[0], adjoint_pair[1], precision=highest) + jnp.dot(trans_pair[1], adjoint_pair[0], precision=highest)
    return jnp.stack([real_part, imag_part], axis=1).astype(jnp.bfloat16)

def reference(transfer, adjoint, lower_rows, pivot_store, owners, inverse_factor):
    spectra = lax.map(spectrum, (transfer, adjoint))
    table = make_table(NT, NF)
    hessian = jnp.einsum('qtk,ksqc->stc', table.astype(jnp.float32), spectra.astype(jnp.float32), precision=lax.Precision.HIGHEST)
    hessian = hessian.reshape(NS * NT, C)
    blocks = []
    for panel_index in range(PANELS):
        row_start = (owners[panel_index] * C).astype(jnp.int32)
        col_start = jnp.asarray(panel_index * C).astype(jnp.int32)
        blocks.append(lax.dynamic_slice(pivot_store, (row_start, col_start), (C, C)))
    pivots = jnp.concatenate(blocks, axis=1)
    update = lax.dot_general(lower_rows, pivots, (((1,), (1,)), ((), ())), preferred_element_type=jnp.float32)
    reduced = (hessian - update).astype(jnp.bfloat16)
    return jnp.dot(reduced, inverse_factor, preferred_element_type=jnp.float32).astype(jnp.bfloat16)
```

```python
import functools
import math

import jax
import jax.numpy as jnp
from jax import lax
from jax.experimental import pallas as pl
from jax.experimental.pallas import tpu as pltpu
from jax.sharding import PartitionSpec as P

MESH = pl.DeviceIdType.MESH
CHUNK = 8
AHEAD = 3
COARSE = 32


def flip(me, mask):
    bit = 1
    other = me
    while bit <= mask:
        if mask & bit:
            other = other + bit * (1 - 2 * lax.rem(me // bit, 2))
        bit *= 2
    return other


def kernel(
    nf, ng, kc,
    owners_ref, tr_hbm, ad_hbm, lo_hbm, pv_hbm, out_ref,
    tr, ad, lo, pv, spec, sbuf, rbuf, table, acc,
    in_sem, lo_sem, pv_sem, own_sem, send_sem, recv_sem, psend_sem, precv_sem,
):
    kl, _, sl, _ = tr.shape
    c = ad.shape[3]
    nch = kl // kc
    s_loc = sl // nf
    nt, width = acc.shape
    me = lax.axis_index("freq")
    grp = lax.axis_index("grp")

    barrier = pltpu.get_barrier_semaphore()
    for mask in range(1, nf):
        pl.semaphore_signal(barrier, inc=1, device_id={"freq": flip(me, mask)}, device_id_type=MESH)
    for mask in range(1, ng):
        pl.semaphore_signal(barrier, inc=1, device_id={"grp": flip(grp, mask)}, device_id_type=MESH)

    def loads(j):
        rows = pl.ds(j * kc, kc)
        return (
            pltpu.make_async_copy(tr_hbm.at[rows], tr.at[rows], in_sem.at[j, 0]),
            pltpu.make_async_copy(ad_hbm.at[rows], ad.at[rows], in_sem.at[j, 1]),
        )

    lo_copy = pltpu.make_async_copy(lo_hbm, lo, lo_sem)
    pv_copy = pltpu.make_async_copy(pv_hbm, pv.at[grp], pv_sem)

    for j in range(min(AHEAD, nch)):
        for copy in loads(j):
            copy.start()

    def spectra(j):
        for copy in loads(j):
            copy.wait()
        for i in range(kc):
            k = j * kc + i
            right = jnp.concatenate([ad[k, 0], ad[k, 1]], axis=1)
            left = jnp.concatenate([tr[k, 0], tr[k, 1]], axis=0)
            both = jnp.dot(left, right, preferred_element_type=jnp.float32)
            spec[0, pl.ds(i * sl, sl), :] = both[:sl, :c] - both[sl:, c:]
            spec[1, pl.ds(i * sl, sl), :] = both[:sl, c:] + both[sl:, :c]
        for d in range(nf):
            for s in range(s_loc):
                rows = pl.ds(d * s_loc + s, kc, stride=sl)
                block = jnp.concatenate([spec[0, rows, :], spec[1, rows, :]], axis=0)
                sbuf[j, d, :, s * c:(s + 1) * c] = block.astype(jnp.bfloat16)

    def own_copy(j):
        return pltpu.make_async_copy(sbuf.at[j, me], rbuf.at[j, me], own_sem.at[j])

    def remote(j, mask):
        return pltpu.make_async_remote_copy(
            src_ref=sbuf.at[j, flip(me, mask)],
            dst_ref=rbuf.at[j, me],
            send_sem=send_sem.at[j, mask],
            recv_sem=recv_sem.at[j, mask],
            device_id={"freq": flip(me, mask)},
            device_id_type=MESH,
        )

    def arrival(j, mask):
        other = flip(me, mask)
        return pltpu.make_async_remote_copy(
            src_ref=sbuf.at[j, other],
            dst_ref=rbuf.at[j, other],
            send_sem=send_sem.at[j, mask],
            recv_sem=recv_sem.at[j, mask],
            device_id={"freq": other},
            device_id_type=MESH,
        )

    def pivot_copy(mask, slot):
        return pltpu.make_async_remote_copy(
            src_ref=pv_hbm,
            dst_ref=pv.at[slot],
            send_sem=psend_sem.at[mask],
            recv_sem=precv_sem.at[mask],
            device_id={"grp": flip(grp, mask)},
            device_id_type=MESH,
        )

    def send(j):
        for mask in range(nf - 1, 0, -1):
            remote(j, mask).start()
        own_copy(j).start()

    spectra(0)
    pl.semaphore_wait(barrier, nf - 1 + ng - 1)
    send(0)

    @pl.loop(1, nch)
    def _(j):
        @pl.when(j + AHEAD - 1 < nch)
        def _():
            for copy in loads(j + AHEAD - 1):
                copy.start()

        spectra(j)
        send(j)

    pv_copy.start()
    lo_copy.start()
    for mask in range(1, ng):
        pivot_copy(mask, grp).start()

    cols = nf * 2 * kc
    coarse = nt // COARSE
    scale = 1.0 / math.sqrt(kl * nf)
    turn = 2.0 * math.pi / nt

    @pl.loop(0, nch)
    def _(j):
        def phase(rows, step, shift):
            col = lax.broadcasted_iota(jnp.int32, (rows, cols), 1)
            row = lax.broadcasted_iota(jnp.int32, (rows, cols), 0) * step
            kk = (col // (2 * kc)) * kl + j * kc + col % kc
            q = (col // kc) % 2
            whole = kk * row + q * shift
            return (whole % nt).astype(jnp.float32) * turn

        high = phase(coarse, COARSE, 0)
        low = phase(COARSE, 1, nt // 4)
        cos_high, sin_high = jnp.cos(high) * scale, jnp.sin(high) * scale
        cos_low, sin_low = jnp.cos(low), jnp.sin(low)
        for a in range(coarse):
            value = cos_high[a:a + 1] * cos_low - sin_high[a:a + 1] * sin_low
            table[j, a * COARSE:(a + 1) * COARSE, :] = value.astype(jnp.bfloat16)

    lo_copy.wait()
    pv_copy.wait()
    for mask in range(1, ng):
        pivot_copy(mask, flip(grp, mask)).wait_recv()
    panels = lo.shape[1] // c
    pivots = jnp.concatenate(
        [pv[owners_ref[p], :, p * c:(p + 1) * c] for p in range(panels)], axis=1
    )
    tile = min(256, nt)

    for s in range(s_loc):
        @pl.loop(0, nt // tile)
        def _(i):
            rows = lo[pl.ds(pl.multiple_of(s * nt + i * tile, tile), tile), :]
            update = lax.dot_general(
                rows, pivots, (((1,), (1,)), ((), ())), preferred_element_type=jnp.float32
            )
            acc[pl.ds(pl.multiple_of(i * tile, tile), tile), s * c:(s + 1) * c] = -update

    def arrive(j):
        for mask in range(nf - 1, 0, -1):
            arrival(j, mask).wait_recv()
        own_copy(j).wait()

    def term(j, i):
        rows = pl.ds(pl.multiple_of(i * tile, tile), tile)
        right = rbuf[j].reshape(cols, width)
        return acc[rows, :] + jnp.dot(table[j, rows, :], right, preferred_element_type=jnp.float32)

    @pl.loop(0, nch - 1)
    def _(j):
        arrive(j)

        @pl.loop(0, nt // tile)
        def _(i):
            acc[pl.ds(pl.multiple_of(i * tile, tile), tile), :] = term(j, i)

    last = nch - 1
    arrive(last)

    @pl.loop(0, nt // tile)
    def _(i):
        value = term(last, i).astype(jnp.bfloat16)
        for s in range(s_loc):
            out_ref[pl.ds(pl.multiple_of(s * nt + i * tile, tile), tile), :] = value[:, s * c:(s + 1) * c]

    @pl.loop(0, nch)
    def _(j):
        for mask in range(nf - 1, 0, -1):
            remote(j, mask).wait_send()

    for mask in range(1, ng):
        pivot_copy(mask, grp).wait_send()


def per_device(nf, ng, transfer, adjoint, lower_rows, pivot_store, owners, inverse_factor):
    kl, _, sl, m = transfer.shape
    c = adjoint.shape[3]
    kc = min(CHUNK, kl)
    nch = kl // kc
    s_loc = sl // nf
    rows = lower_rows.shape[0]
    nt = rows // s_loc
    bf16 = jnp.bfloat16
    reduced = pl.pallas_call(
        functools.partial(kernel, nf, ng, kc),
        out_shape=jax.ShapeDtypeStruct((rows, c), bf16),
        in_specs=[pl.BlockSpec(memory_space=pltpu.SMEM)] + [pl.BlockSpec(memory_space=pl.ANY)] * 4,
        out_specs=pl.BlockSpec(memory_space=pltpu.VMEM),
        scratch_shapes=[
            pltpu.VMEM(transfer.shape, bf16),
            pltpu.VMEM(adjoint.shape, bf16),
            pltpu.VMEM(lower_rows.shape, bf16),
            pltpu.VMEM((ng,) + pivot_store.shape, bf16),
            pltpu.VMEM((2, kc * sl, c), jnp.float32),
            pltpu.VMEM((nch, nf, 2 * kc, s_loc * c), bf16),
            pltpu.VMEM((nch, nf, 2 * kc, s_loc * c), bf16),
            pltpu.VMEM((nch, nt, nf * 2 * kc), bf16),
            pltpu.VMEM((nt, s_loc * c), jnp.float32),
            pltpu.SemaphoreType.DMA((nch, 2)),
            pltpu.SemaphoreType.DMA,
            pltpu.SemaphoreType.DMA,
            pltpu.SemaphoreType.DMA((nch,)),
            pltpu.SemaphoreType.DMA((nch, nf)),
            pltpu.SemaphoreType.DMA((nch, nf)),
            pltpu.SemaphoreType.DMA((ng,)),
            pltpu.SemaphoreType.DMA((ng,)),
        ],
        compiler_params=pltpu.CompilerParams(
            collective_id=0, has_side_effects=True, vmem_limit_bytes=52 * 1024 * 1024
        ),
    )(owners, transfer, adjoint, lower_rows, pivot_store)
    return jnp.dot(reduced, inverse_factor, preferred_element_type=jnp.float32).astype(bf16)


def solution(mesh):
    nf, ng = mesh.shape["freq"], mesh.shape["grp"]
    in_specs = (
        P("freq", None, "grp", None),
        P("freq", None, None, None),
        P(("grp", "freq"), None),
        P("grp", None),
        P(),
        P(),
    )
    out_specs = P(("grp", "freq"), None)
    return jax.shard_map(
        functools.partial(per_device, nf, ng),
        mesh=mesh, in_specs=in_specs, out_specs=out_specs, check_vma=False,
    )
```

```python
import functools
import math

import jax
import jax.numpy as jnp
from jax import lax
from jax.experimental import pallas as pl
from jax.experimental.pallas import tpu as pltpu
from jax.sharding import PartitionSpec as P

MESH = pl.DeviceIdType.MESH
CHUNK = 8
AHEAD = 3
TILE = 1024
VMEM_BYTES = 64 * 1024 * 1024
SPARE = 11 * 1024 * 1024
COARSE = 32


def flip(me, mask):
    bit = 1
    other = me
    while bit <= mask:
        if mask & bit:
            other = other + bit * (1 - 2 * lax.rem(me // bit, 2))
        bit *= 2
    return other


def kernel(
    nf, ng, kc,
    owners_hbm, tr_hbm, ad_hbm, lo_hbm, pv_hbm, out_ref,
    owners, tr, ad, lo, pv, spec, sbuf, rbuf, table, acc,
    in_sem, owners_sem, lo_sem, pv_sem, own_sem, send_sem, recv_sem, psend_sem, precv_sem,
):
    kl, _, sl, _ = tr.shape
    c = ad.shape[3]
    nch = kl // kc
    s_loc = sl // nf
    nt, width = acc.shape
    me = lax.axis_index("freq")
    grp = lax.axis_index("grp")

    def loads(j):
        rows = pl.ds(j * kc, kc)
        return (
            pltpu.make_async_copy(tr_hbm.at[rows], tr.at[rows], in_sem.at[j, 0]),
            pltpu.make_async_copy(ad_hbm.at[rows], ad.at[rows], in_sem.at[j, 1]),
        )

    lo_copy = pltpu.make_async_copy(lo_hbm, lo, lo_sem)
    owners_copy = pltpu.make_async_copy(owners_hbm, owners, owners_sem)
    pv_copy = pltpu.make_async_copy(pv_hbm, pv.at[grp], pv_sem)

    for copy in loads(0):
        copy.start()

    barrier = pltpu.get_barrier_semaphore()
    for mask in range(1, nf):
        pl.semaphore_signal(barrier, inc=1, device_id={"freq": flip(me, mask)}, device_id_type=MESH)
    for mask in range(1, ng):
        pl.semaphore_signal(barrier, inc=1, device_id={"grp": flip(grp, mask)}, device_id_type=MESH)

    def spectra(j):
        for i in range(kc):
            k = j * kc + i
            right = jnp.concatenate([ad[k, 0], ad[k, 1]], axis=1)
            left = jnp.concatenate([tr[k, 0], tr[k, 1]], axis=0)
            both = jnp.dot(left, right, preferred_element_type=jnp.float32)
            spec[0, pl.ds(i * sl, sl), :] = both[:sl, :c] - both[sl:, c:]
            spec[1, pl.ds(i * sl, sl), :] = both[:sl, c:] + both[sl:, :c]
        for d in range(nf):
            for s in range(s_loc):
                rows = pl.ds(d * s_loc + s, kc, stride=sl)
                block = jnp.concatenate([spec[0, rows, :], spec[1, rows, :]], axis=0)
                sbuf[j, d, :, s * c:(s + 1) * c] = block.astype(jnp.bfloat16)

    def own_copy(j):
        return pltpu.make_async_copy(sbuf.at[j, me], rbuf.at[j, me], own_sem.at[j])

    def remote(j, mask):
        return pltpu.make_async_remote_copy(
            src_ref=sbuf.at[j, flip(me, mask)],
            dst_ref=rbuf.at[j, me],
            send_sem=send_sem.at[j, mask],
            recv_sem=recv_sem.at[j, mask],
            device_id={"freq": flip(me, mask)},
            device_id_type=MESH,
        )

    def arrival(j, mask):
        other = flip(me, mask)
        return pltpu.make_async_remote_copy(
            src_ref=sbuf.at[j, other],
            dst_ref=rbuf.at[j, other],
            send_sem=send_sem.at[j, mask],
            recv_sem=recv_sem.at[j, mask],
            device_id={"freq": other},
            device_id_type=MESH,
        )

    def pivot_copy(mask, slot):
        return pltpu.make_async_remote_copy(
            src_ref=pv_hbm,
            dst_ref=pv.at[slot],
            send_sem=psend_sem.at[mask],
            recv_sem=precv_sem.at[mask],
            device_id={"grp": flip(grp, mask)},
            device_id_type=MESH,
        )

    far = tuple(range(nf - 1, nf // 2 - 1, -1))
    near = tuple(range(nf // 2 - 1, 0, -1))
    def send(j, masks):
        for mask in masks:
            remote(j, mask).start()
        own_copy(j).start()

    for copy in loads(0):
        copy.wait()
    for j in range(1, min(AHEAD, nch)):
        for copy in loads(j):
            copy.start()
    spectra(0)
    pl.semaphore_wait(barrier, nf - 1 + ng - 1)
    send(0, far + near)

    @pl.loop(1, nch)
    def _(j):
        @pl.when(j + AHEAD - 1 < nch)
        def _():
            for copy in loads(j + AHEAD - 1):
                copy.start()

        for copy in loads(j):
            copy.wait()
        spectra(j)
        send(j, near + far)

    owners_copy.start()
    pv_copy.start()
    lo_copy.start()
    for mask in range(1, ng):
        pivot_copy(mask, grp).start()

    cols = nf * 2 * kc
    coarse = nt // COARSE
    scale = 1.0 / math.sqrt(kl * nf)
    turn = 2.0 * math.pi / nt

    @pl.loop(0, nch)
    def _(j):
        def phase(rows, step, shift):
            col = lax.broadcasted_iota(jnp.int32, (rows, cols), 1)
            row = lax.broadcasted_iota(jnp.int32, (rows, cols), 0) * step
            kk = (col // (2 * kc)) * kl + j * kc + col % kc
            q = (col // kc) % 2
            whole = kk * row + q * shift
            return (whole % nt).astype(jnp.float32) * turn

        high = phase(coarse, COARSE, 0)
        low = phase(COARSE, 1, nt // 4)
        cos_high, sin_high = jnp.cos(high) * scale, jnp.sin(high) * scale
        cos_low, sin_low = jnp.cos(low), jnp.sin(low)
        for a in range(coarse):
            value = cos_high[a:a + 1] * cos_low - sin_high[a:a + 1] * sin_low
            table[j, a * COARSE:(a + 1) * COARSE, :] = value.astype(jnp.bfloat16)

    lo_copy.wait()
    owners_copy.wait()
    pv_copy.wait()
    for mask in range(1, ng):
        pivot_copy(mask, flip(grp, mask)).wait_recv()
    panels = lo.shape[1] // c
    pivots = jnp.concatenate(
        [pv[owners[p], :, p * c:(p + 1) * c] for p in range(panels)], axis=1
    )
    tile = min(TILE, nt)

    for s in range(s_loc):
        @pl.loop(0, nt // tile)
        def _(i):
            rows = lo[pl.ds(pl.multiple_of(s * nt + i * tile, tile), tile), :]
            update = lax.dot_general(
                rows, pivots, (((1,), (1,)), ((), ())), preferred_element_type=jnp.float32
            )
            acc[pl.ds(pl.multiple_of(i * tile, tile), tile), s * c:(s + 1) * c] = -update

    def arrive(j):
        for mask in range(nf - 1, 0, -1):
            arrival(j, mask).wait_recv()
        own_copy(j).wait()

    def term(j, i):
        rows = pl.ds(pl.multiple_of(i * tile, tile), tile)
        right = rbuf[j].reshape(cols, width)
        return acc[rows, :] + jnp.dot(table[j, rows, :], right, preferred_element_type=jnp.float32)

    @pl.loop(0, nch - 1)
    def _(j):
        arrive(j)

        @pl.loop(0, nt // tile)
        def _(i):
            acc[pl.ds(pl.multiple_of(i * tile, tile), tile), :] = term(j, i)

    last = nch - 1
    arrive(last)

    @pl.loop(0, nt // tile)
    def _(i):
        value = term(last, i).astype(jnp.bfloat16)
        for s in range(s_loc):
            out_ref[pl.ds(pl.multiple_of(s * nt + i * tile, tile), tile), :] = value[:, s * c:(s + 1) * c]

    @pl.loop(0, nch)
    def _(j):
        for mask in range(nf - 1, 0, -1):
            remote(j, mask).wait_send()

    for mask in range(1, ng):
        pivot_copy(mask, grp).wait_send()


def per_device(nf, ng, transfer, adjoint, lower_rows, pivot_store, owners, inverse_factor):
    kl, _, sl, m = transfer.shape
    c = adjoint.shape[3]
    kc = min(CHUNK, kl)
    nch = kl // kc
    s_loc = sl // nf
    rows = lower_rows.shape[0]
    nt = rows // s_loc
    bf16 = jnp.bfloat16
    in_hbm = lambda x: pltpu.with_memory_space_constraint(x, pltpu.HBM)
    reduced = pl.pallas_call(
        functools.partial(kernel, nf, ng, kc),
        out_shape=jax.ShapeDtypeStruct((rows, c), bf16),
        in_specs=[pl.BlockSpec(memory_space=pltpu.HBM)] * 5,
        out_specs=pl.BlockSpec(memory_space=pltpu.VMEM),
        scratch_shapes=[
            pltpu.SMEM(owners.shape, jnp.int32),
            pltpu.VMEM(transfer.shape, bf16),
            pltpu.VMEM(adjoint.shape, bf16),
            pltpu.VMEM(lower_rows.shape, bf16),
            pltpu.VMEM((ng,) + pivot_store.shape, bf16),
            pltpu.VMEM((2, kc * sl, c), jnp.float32),
            pltpu.VMEM((nch, nf, 2 * kc, s_loc * c), bf16),
            pltpu.VMEM((nch, nf, 2 * kc, s_loc * c), bf16),
            pltpu.VMEM((nch, nt, nf * 2 * kc), bf16),
            pltpu.VMEM((nt, s_loc * c), jnp.float32),
            pltpu.SemaphoreType.DMA((nch, 2)),
            pltpu.SemaphoreType.DMA,
            pltpu.SemaphoreType.DMA,
            pltpu.SemaphoreType.DMA,
            pltpu.SemaphoreType.DMA((nch,)),
            pltpu.SemaphoreType.DMA((nch, nf)),
            pltpu.SemaphoreType.DMA((nch, nf)),
            pltpu.SemaphoreType.DMA((ng,)),
            pltpu.SemaphoreType.DMA((ng,)),
        ],
        compiler_params=pltpu.CompilerParams(
            collective_id=0, has_side_effects=True, vmem_limit_bytes=VMEM_BYTES - 2 * rows * c - SPARE
        ),
    )(in_hbm(owners), transfer, adjoint, lower_rows, in_hbm(pivot_store))
    return jnp.dot(reduced, inverse_factor, preferred_element_type=jnp.float32).astype(bf16)


def solution(mesh):
    nf, ng = mesh.shape["freq"], mesh.shape["grp"]
    in_specs = (
        P("freq", None, "grp", None),
        P("freq", None, None, None),
        P(("grp", "freq"), None),
        P("grp", None),
        P(),
        P(),
    )
    out_specs = P(("grp", "freq"), None)
    return jax.shard_map(
        functools.partial(per_device, nf, ng),
        mesh=mesh, in_specs=in_specs, out_specs=out_specs, check_vma=False,
    )
```
